32 devices in a mesh: dom: 16 (over z, x, core), col: 2 (over y).
Axes of the slice: x: 2, y: 2, z: 4, core: 2. Of those that a mesh axis runs over, the one named last changes fastest.
Arguments:
- feats: bfloat16 [8192, 256], P('dom', 'col'), may hold values from -6 to 6
- w_first: bfloat16 [256, 256], replicated, may hold values from -0.375 to 0.375
- w_second: bfloat16 [256, 256], replicated, may hold values from -0.375 to 0.375
- block_cols: int32 [64, 32], P('dom'), may hold values from 0 to 63, as said below
- block_count: int32 [64], P('dom'), may hold values from 1 to 32
- block_vals: bfloat16 [64, 32, 128, 128], P('dom', 'col'), may hold values from -0.125 to 0.125
- cotangent: bfloat16 [8192, 256], P('dom', 'col'), may hold values from -6 to 6
Outputs:
- output: float32 [8192, 256], P('dom', 'col')
- grad_first: float32 [256, 256], P(None, 'col')
- grad_second: float32 [256, 256], P(None, 'col')
The draws below stay inside these ranges and needn't reach their ends.
Inputs may be any that keep to these rules, and one draw needn't show every extreme that they name: Each row of block_cols names 32 different column blocks.
All inputs are finite; a program needn't handle non-finite values.
Results may differ from the reference program's by a relative error of at most 0.019.
Values may be sent and summed in bfloat16 or wider, within the bound.
No kernel may reach another device: no remote copies, remote signals or barrier semaphores. Data moves between devices by JAX's collectives and lax.ppermute only.
A program may use at most 64 MiB of HBM per device.

```python
import jax
import jax.numpy as jnp
from jax import lax

F = 256
BLK = 128
KMAX = 32
NBLK = 64
NODES = 8192


def draw_block_cols(key, part):
    row_ids = jnp.arange(NBLK, dtype=jnp.int32)[:, None]
    col_ids = jnp.arange(NBLK, dtype=jnp.int32)[None, :]
    distance = jnp.minimum((col_ids - row_ids) % NBLK, (row_ids - col_ids) % NBLK)
    inband = (distance <= 16).astype(jnp.int32)
    noise = jax.random.randint(jax.random.fold_in(key, 11), (NBLK, NBLK), 0, 1 << 16)
    base = noise * NBLK + col_ids
    near_scores = inband * (1 << 28) + base
    far_scores = (1 - inband) * (1 << 28) + base
    near_vals, near_cols = lax.top_k(near_scores, KMAX - 4)
    far_vals, far_cols = lax.top_k(far_scores, 4)
    return jnp.concatenate([near_cols, far_cols], axis=1).astype(jnp.int32)


def draw_block_count(key, part):
    first_key = jax.random.fold_in(key, 21)
    second_key = jax.random.fold_in(key, 22)
    counts = jax.random.randint(first_key, (NBLK,), 1, KMAX + 1)
    where_full = jax.random.randint(second_key, (), 0, NBLK)
    counts = counts.at[where_full].set(KMAX)
    return counts.astype(jnp.int32)


def block_scale(rng, dims, split, low, top_value):
    loudness, own = 1.0, jax.random.fold_in(rng, 6)
    for position, parts in split:
        draws = jnp.exp(jax.random.uniform(jax.random.fold_in(own, position), (parts,), jnp.float32, low / len(split), top_value / len(split)))
        loudness = loudness * jnp.repeat(draws, dims[position] // parts).reshape([-1 if axis == position else 1 for axis in range(len(dims))])
    return loudness


def gaussian(stream_key, extent, scale, reach, cuts=(), kind=jnp.bfloat16):
    level = block_scale(stream_key, extent, cuts, -0.22, 0.18) if cuts else 1.0
    drawn = jax.random.normal(stream_key, extent, jnp.float32) * scale * level
    return jnp.minimum(jnp.maximum(drawn, -reach), reach).astype(kind)


def setup_inputs(seed: int = 0) -> dict:
    keys = jax.random.split(jax.random.key(seed), 8)
    feats = gaussian(keys[0], (NODES, F), 1.0, 6.0, ((0, 16), (1, 2)))
    w_first = gaussian(keys[1], (F, F), F ** -0.5, 0.375)
    w_second = gaussian(keys[2], (F, F), F ** -0.5, 0.375)
    block_cols = draw_block_cols(jax.random.fold_in(keys[7], 71), 0)
    block_count = draw_block_count(jax.random.fold_in(keys[7], 71), 0)
    block_vals = gaussian(keys[5], (NBLK, KMAX, BLK, BLK), (BLK * KMAX // 2) ** -0.5, 0.125, ((0, 16), (1, 2)))
    cotangent = gaussian(keys[6], (NODES, F), 1.0, 6.0, ((0, 16), (1, 2)))
    return {"feats": feats, "w_first": w_first, "w_second": w_second, "block_cols": block_cols, "block_count": block_count, "block_vals": block_vals, "cotangent": cotangent}


def aggregate(prod, block_cols, block_count, block_vals):
    blocks = prod.reshape(NBLK, BLK, F)
    slots = jnp.arange(KMAX)

    def one_row(args):
        cols, count, vals = args
        picked = blocks[cols].astype(jnp.float32)
        mask = (slots < count).astype(jnp.float32)
        return jnp.einsum('kij,kjf->if', vals.astype(jnp.float32) * mask[:, None, None], picked)

    return lax.map(one_row, (block_cols, block_count, block_vals)).reshape(NBLK * BLK, F)


def transpose(grad, block_cols, block_count, block_vals):
    rowgrad = grad.reshape(NBLK, BLK, F).astype(jnp.float32)
    slots = jnp.arange(KMAX)

    def step(total, args):
        cols, count, vals, piece = args
        mask = (slots < count).astype(jnp.float32)
        term = jnp.einsum('kij,if->kjf', vals.astype(jnp.float32) * mask[:, None, None], piece)
        return total.at[cols].add(term), None

    total, unused = lax.scan(step, jnp.zeros((NBLK, BLK, F), jnp.float32), (block_cols, block_count, block_vals, rowgrad))
    return total.reshape(NBLK * BLK, F)


def reference(feats, w_first, w_second, block_cols, block_count, block_vals, cotangent):
    proj_first = jnp.dot(feats, w_first, preferred_element_type=jnp.float32).astype(jnp.bfloat16)
    first = aggregate(proj_first, block_cols, block_count, block_vals)
    hidden = (first * jax.nn.sigmoid(first)).astype(jnp.bfloat16)
    proj_second = jnp.dot(hidden, w_second, preferred_element_type=jnp.float32).astype(jnp.bfloat16)
    output = aggregate(proj_second, block_cols, block_count, block_vals)
    back_second = transpose(cotangent, block_cols, block_count, block_vals).astype(jnp.bfloat16)
    grad_second = jnp.dot(hidden.T, back_second, preferred_element_type=jnp.float32)
    hidden_grad = jnp.dot(back_second, w_second.T, preferred_element_type=jnp.float32)
    sig = jax.nn.sigmoid(first)
    act_grad = (hidden_grad * (sig + first * sig * (1.0 - sig))).astype(jnp.bfloat16)
    back_first = transpose(act_grad, block_cols, block_count, block_vals).astype(jnp.bfloat16)
    grad_first = jnp.dot(feats.T, back_first, preferred_element_type=jnp.float32)
    return (output, grad_first, grad_second)
```

```python
import functools

import jax
import jax.numpy as jnp
from jax import lax
from jax.experimental import pallas as pl
from jax.experimental.pallas import tpu as pltpu
from jax.sharding import PartitionSpec as P

BLK = 128
GROUP = 4
LANES = 128
F32 = jnp.float32
BF16 = jnp.bfloat16


def swap(value, axis, mask):
    size = lax.axis_size(axis)
    return lax.ppermute(value, axis, [(i, i ^ mask) for i in range(size)])


def join(pieces):
    if pieces[0].shape[1] % LANES:
        return [jnp.concatenate(pieces, axis=1)]
    return list(pieces)


def gather(own):
    nd, nc = lax.axis_size("dom"), lax.axis_size("col")
    far = range(4, nd, 4)
    got = {(0, 0): own}
    for v in far:
        got[v, 0] = swap(own, "dom", v)
    for n, v in enumerate((0, *far)):
        for cx in range(1, nc):
            got[v, cx] = swap(got[v, 0], "col", cx)
        if nd >= 4:
            got[v | 2, 0] = swap(got[v, 0], "dom", 2)
            for cx in range(1, nc):
                if (n + cx) % 2:
                    got[v | 2, cx] = swap(got[v, cx], "dom", 2)
                else:
                    got[v | 2, cx] = swap(got[v | 2, 0], "col", cx)
    return [join([got[v, cx] for cx in range(nc)]) for v in range(0, nd, 2)]


def load(groups, dest, sems, first=0):
    copies = []
    for g, pieces in enumerate(groups):
        lane = 0
        for piece in pieces:
            rows, wide = piece.shape
            copies.append(
                pltpu.make_async_copy(
                    piece,
                    dest.at[pl.ds(g * rows, rows), pl.ds(lane, wide)],
                    sems.at[first + len(copies)],
                )
            )
            lane += wide
    for copy in copies:
        copy.start()
    return copies


def split(refs, counts):
    out, at = [], 0
    for n in counts:
        out.append(refs[at : at + n])
        at += n
    return out, refs[at:]


def back_kernel(nb, slots, counts, me, idx, w2, v_own, v_far, *refs):
    groups, (lk, lx, ln, hg, cot, cw, sems) = split(refs, counts)
    rows = nb * BLK
    copies = load(groups, cot, sems)
    dom = me[0]
    stride = slots + GROUP
    blank = hg.shape[0] // BLK
    hg[...] = jnp.zeros_like(hg)
    for r in range(2 * nb):

        def scan(k, n, r=r):
            b = idx[r * slots + k]
            rel = (jnp.maximum(b, 0) // nb) ^ dom
            ok = jnp.logical_and(b >= 0, (rel & 1) == 0)
            lk[r * stride + n] = k
            lx[r * stride + n] = (rel >> 1) * nb + jnp.maximum(b, 0) % nb
            return n + ok.astype(jnp.int32)

        n = lax.fori_loop(0, slots, scan, jnp.int32(0))
        ln[r] = n
        for t in range(GROUP):
            lk[r * stride + n + t] = 0
            lx[r * stride + n + t] = blank
    for copy in copies:
        copy.wait()
    cw[...] = lax.dot_general(
        cot[...], w2[...], (((1,), (1,)), ((), ())), preferred_element_type=F32
    ).astype(BF16)
    for r in range(2 * nb):
        vals = v_own if r < nb else v_far
        grad = cw[r * BLK : (r + 1) * BLK, :]

        def add(n, carry, r=r, vals=vals, grad=grad):
            tile = vals[r % nb, lk[r * stride + n]]
            at = pl.ds(pl.multiple_of(lx[r * stride + n] * BLK, BLK), BLK)
            hg[at, :] += lax.dot_general(
                tile, grad, (((0,), (0,)), ((), ())), preferred_element_type=F32
            )
            return carry

        lax.fori_loop(0, ln[r], add, 0)


def rows_product(nb, slots, r, lk, lx, ln, vals, source, width):
    stride = slots + GROUP

    def step(g, acc):
        at = r * stride + g * GROUP
        left = jnp.concatenate([vals[r % nb, lk[at + t]] for t in range(GROUP)], axis=1)
        right = jnp.concatenate(
            [
                source[pl.ds(pl.multiple_of(lx[at + t] * BLK, BLK), BLK), :]
                for t in range(GROUP)
            ],
            axis=0,
        )
        return acc + jnp.dot(left, right, preferred_element_type=F32)

    steps = (ln[r] + GROUP - 1) // GROUP
    return lax.fori_loop(0, steps, step, jnp.zeros((BLK, width), F32))


def first_kernel(nb, slots, counts, lk, lx, ln, v_own, v_far, *refs):
    groups, (keep, send, src, sems) = split(refs, counts)
    copies = load(groups, src, sems)
    width = src.shape[1]
    src[src.shape[0] - BLK :, :] = jnp.zeros((BLK, width), BF16)
    for copy in copies:
        copy.wait()
    for r in range(2 * nb):
        acc = rows_product(nb, slots, r, lk, lx, ln, v_own if r < nb else v_far, src, width)
        if r < nb:
            keep[r * BLK : (r + 1) * BLK, :] = acc
        else:
            send[(r - nb) * BLK : (r - nb + 1) * BLK, :] = acc.astype(BF16)


def second_kernel(nb, slots, counts, n_cot, me, lk, lx, ln, w1, w2, v_own, v_far, hg, *refs):
    groups, (keep, send, gkeep, gsend, agg, hid, cot, mix, gf, sems) = split(refs, counts)
    copies = load(groups[:-2], agg, sems)
    more = load(groups[-2:], cot, sems, len(copies))
    blocks, width = agg.shape[0], agg.shape[1]
    narrow = gkeep.shape[2]
    parts = width // narrow
    chunk = nb * BLK
    hid[blocks:, :] = jnp.zeros((BLK, width), BF16)
    for copy in copies:
        copy.wait()
    gf[...] = jnp.zeros_like(gf)
    for g in range(blocks // chunk):
        rows = pl.ds(g * chunk, chunk)
        a = agg[rows, :]
        first = jnp.dot(a, w1[...], preferred_element_type=F32)
        sig = 0.5 * jnp.tanh(0.5 * first) + 0.5
        act = first * sig
        hid[rows, :] = act.astype(BF16)
        slope = sig + act * (1.0 - sig)
        grad = (hg[rows, :] * slope).astype(BF16)
        gf[...] += lax.dot_general(
            a, grad, (((0,), (0,)), ((), ())), preferred_element_type=F32
        )
    for r in range(2 * nb):
        acc = rows_product(nb, slots, r, lk, lx, ln, v_own if r < nb else v_far, hid, width)
        mix[r * BLK : (r + 1) * BLK, :] = acc.astype(BF16)
    keep[...] = jnp.dot(mix[:chunk, :], w2[...], preferred_element_type=F32)
    send[...] = jnp.dot(mix[chunk:, :], w2[...], preferred_element_type=F32).astype(BF16)
    for copy in more:
        copy.wait()
    gs = lax.dot_general(
        mix[...], cot[...], (((0,), (0,)), ((), ())), preferred_element_type=F32
    )
    col = me[1]
    for which, total in enumerate((gf[...], gs)):
        for p in range(parts):
            at = pl.ds(pl.multiple_of((col ^ p) * narrow, narrow), narrow)
            rows = total[p * narrow : (p + 1) * narrow, :]
            gkeep[which, at, :] = rows[:, :narrow]
            for q in range(1, parts):
                gsend[q - 1, which, at, :] = rows[
                    :, q * narrow : (q + 1) * narrow
                ].astype(BF16)


def any_spec():
    return pl.BlockSpec(memory_space=pl.ANY)


def vmem():
    return pl.BlockSpec(memory_space=pltpu.VMEM)


def smem():
    return pl.BlockSpec(memory_space=pltpu.SMEM)


def params():
    return pltpu.CompilerParams(vmem_limit_bytes=40 << 20)


def body(feats, w_first, w_second, block_cols, block_count, block_vals, cotangent):
    nd, nc = lax.axis_size("dom"), lax.axis_size("col")
    dom, col = lax.axis_index("dom"), lax.axis_index("col")
    rows, narrow = feats.shape
    nb, slots = block_vals.shape[:2]
    width = narrow * nc
    blocks = nd // 2 * rows

    def relative(weight):
        for axis in (0, 1):
            weight = jnp.concatenate(
                [
                    lax.dynamic_slice_in_dim(weight, (col ^ cx) * narrow, narrow, axis)
                    for cx in range(nc)
                ],
                axis=axis,
            )
        return weight

    w1, w2 = relative(w_first), relative(w_second)
    me = jnp.stack([dom, col]).astype(jnp.int32)
    slot_ids = col * slots + jnp.arange(slots)
    cols = lax.dynamic_slice_in_dim(block_cols, col * slots, slots, 1)
    cols = jnp.where(slot_ids[None, :] < block_count[:, None], cols, -1)

    chunks = gather(feats)
    v_own, v_far = block_vals, swap(block_vals, "dom", 1)
    idx = jnp.concatenate([cols, swap(cols, "dom", 1)], axis=0).reshape(-1)
    cot_own = [cotangent] + [swap(cotangent, "col", cx) for cx in range(1, nc)]
    cot_far = [swap(piece, "dom", 1) for piece in cot_own]
    cots = [join(cot_own), join(cot_far)]

    n_list = 2 * nb * (slots + GROUP)
    counts = tuple(len(g) for g in cots)
    lk, lx, ln, hg = pl.pallas_call(
        functools.partial(back_kernel, nb, slots, counts),
        out_shape=(
            jax.ShapeDtypeStruct((n_list,), jnp.int32),
            jax.ShapeDtypeStruct((n_list,), jnp.int32),
            jax.ShapeDtypeStruct((2 * nb,), jnp.int32),
            jax.ShapeDtypeStruct((blocks, width), F32),
        ),
        in_specs=[smem(), smem(), vmem(), vmem(), vmem()] + [any_spec()] * sum(counts),
        out_specs=(smem(), smem(), smem(), vmem()),
        scratch_shapes=[
            pltpu.VMEM((2 * rows, width), BF16),
            pltpu.VMEM((2 * rows, width), BF16),
            pltpu.SemaphoreType.DMA((sum(counts),)),
        ],
        compiler_params=params(),
        name="back",
    )(me, idx, w2, v_own, v_far, *[p for g in cots for p in g])

    counts = tuple(len(g) for g in chunks)
    keep, send = pl.pallas_call(
        functools.partial(first_kernel, nb, slots, counts),
        out_shape=(
            jax.ShapeDtypeStruct((rows, width), F32),
            jax.ShapeDtypeStruct((rows, width), BF16),
        ),
        in_specs=[smem()] * 3 + [vmem()] * 2 + [any_spec()] * sum(counts),
        out_specs=(vmem(), vmem()),
        scratch_shapes=[
            pltpu.VMEM((blocks + BLK, width), BF16),
            pltpu.SemaphoreType.DMA((sum(counts),)),
        ],
        compiler_params=params(),
        name="first",
    )(lk, lx, ln, v_own, v_far, *[p for g in chunks for p in g])

    def reduce_rows(keep, send):
        part = keep + swap(send, "dom", 1).astype(F32)
        total = part[:, :narrow]
        for cx in range(1, nc):
            piece = part[:, cx * narrow : (cx + 1) * narrow].astype(BF16)
            total = total + swap(piece, "col", cx).astype(F32)
        return total

    agg = reduce_rows(keep, send).astype(BF16)
    chunks = gather(agg)
    n_cot = sum(len(g) for g in cots)
    groups = chunks + cots
    counts = tuple(len(g) for g in groups)
    keep, send, gkeep, gsend = pl.pallas_call(
        functools.partial(second_kernel, nb, slots, counts, n_cot),
        out_shape=(
            jax.ShapeDtypeStruct((rows, width), F32),
            jax.ShapeDtypeStruct((rows, width), BF16),
            jax.ShapeDtypeStruct((2, width, narrow), F32),
            jax.ShapeDtypeStruct((nc - 1, 2, width, narrow), BF16),
        ),
        in_specs=[smem()] * 4 + [vmem()] * 5 + [any_spec()] * sum(counts),
        out_specs=(vmem(),) * 4,
        scratch_shapes=[
            pltpu.VMEM((blocks, width), BF16),
            pltpu.VMEM((blocks + BLK, width), BF16),
            pltpu.VMEM((2 * rows, width), BF16),
            pltpu.VMEM((2 * rows, width), BF16),
            pltpu.VMEM((width, width), F32),
            pltpu.SemaphoreType.DMA((sum(counts),)),
        ],
        compiler_params=params(),
        name="second",
    )(me, lk, lx, ln, w1, w2, v_own, v_far, hg, *[p for g in groups for p in g])

    for cx in range(1, nc):
        gkeep = gkeep + swap(gsend[cx - 1], "col", cx).astype(F32)
    even = (dom & 1) == 0
    mine = jnp.where(even, gkeep[0], gkeep[1])
    other = jnp.where(even, gkeep[1], gkeep[0])
    mine = mine + swap(other.astype(BF16), "dom", 1).astype(F32)
    bit = 2
    while bit < nd:
        half = mine.astype(BF16)
        mine = half.astype(F32) + swap(half, "dom", bit).astype(F32)
        bit *= 2
    other = swap(mine, "dom", 1)
    grad_first = jnp.where(even, mine, other)
    grad_second = jnp.where(even, other, mine)
    output = reduce_rows(keep, send)
    return output, grad_first, grad_second


def solution(mesh):
    in_specs = (
        P("dom", "col"),
        P(),
        P(),
        P("dom", None),
        P("dom"),
        P("dom", "col", None, None),
        P("dom", "col"),
    )
    out_specs = (P("dom", "col"), P(None, "col"), P(None, "col"))
    return jax.shard_map(body, mesh=mesh, in_specs=in_specs, out_specs=out_specs, check_vma=False)
```

```python
import functools

import jax
import jax.numpy as jnp
from jax import lax
from jax.experimental import pallas as pl
from jax.experimental.pallas import tpu as pltpu
from jax.sharding import PartitionSpec as P


BLK = 128
GROUP = 4
LANES = 128
F32 = jnp.float32
BF16 = jnp.bfloat16


def swap(value, axis, mask):
    size = lax.axis_size(axis)
    return lax.ppermute(value, axis, [(i, i ^ mask) for i in range(size)])


def widen(own):
    if own.shape[1] % LANES:
        return lax.all_gather(own, "col", axis=1, tiled=True)
    return own


def gather_order(nd, nc):
    far = list(range(4, nd, 4))
    order = [(v, 0, (0, 0), "dom") for v in far[:2]]
    late = [(v, 0, (0, 0), "dom") for v in far[2:]]
    corners = []
    for n, v in enumerate((0, *far)):
        if nd >= 4:
            order.append((v | 2, 0, (v, 0), "dom"))
        order += [(v, cx, (v, 0), "col") for cx in range(1, nc)]
        order += late + corners
        late, corners = [], []
        for cx in range(1, nc):
            if nd >= 4 and (n + cx) % 2:
                corners.append((v | 2, cx, (v, cx), "dom"))
            elif nd >= 4:
                corners.append((v | 2, cx, (v | 2, 0), "col"))
    return order + corners


def gather(own, nc):
    nd = lax.axis_size("dom")
    got = {(0, 0): own}
    for v, cx, (sv, sc), axis in gather_order(nd, nc):
        mask = v ^ sv if axis == "dom" else cx ^ sc
        got[v, cx] = swap(got[sv, sc], axis, mask)
    return [[got[v, cx] for cx in range(nc)] for v in range(0, nd, 2)]


def load(groups, dest, sems, first=0):
    copies = []
    col = lax.axis_index("col")
    for g, pieces in enumerate(groups):
        for cx, piece in enumerate(pieces):
            rows, wide = piece.shape
            lane = 0
            if len(pieces) > 1:
                lane = pl.multiple_of((col ^ cx) * wide, LANES)
            copies.append(
                pltpu.make_async_copy(
                    piece,
                    dest.at[pl.ds(g * rows, rows), pl.ds(lane, wide)],
                    sems.at[first + len(copies)],
                )
            )
    for copy in copies:
        copy.start()
    return copies


def split(refs, counts):
    out, at = [], 0
    for n in counts:
        out.append(refs[at : at + n])
        at += n
    return out, refs[at:]


def tiles(vals, r, lk, at):
    return jnp.concatenate([vals[r, lk[at + t]] for t in range(GROUP)], axis=1)


def place(lx, at):
    return pl.ds(pl.multiple_of(lx[at] * BLK, BLK), BLK)


def back_rows(nb, slots, first, lk, lx, ln, vals, cw, hg):
    for i in range(nb):
        grad = cw[i * BLK : (i + 1) * BLK, :]
        base = (first + i) * (slots + GROUP)

        def step(g, carry, i=i, grad=grad, base=base):
            at = base + g * GROUP
            prod = lax.dot_general(
                tiles(vals, i, lk, at),
                grad,
                (((0,), (0,)), ((), ())),
                preferred_element_type=F32,
            )
            for t in range(GROUP):
                hg[place(lx, at + t), :] += prod[t * BLK : (t + 1) * BLK, :]
            return carry

        lax.fori_loop(0, (ln[first + i] + GROUP - 1) // GROUP, step, 0)


def project(cot, w2, cw):
    cw[...] = lax.dot_general(
        cot[...], w2[...], (((1,), (1,)), ((), ())), preferred_element_type=F32
    ).astype(BF16)


def back_kernel(nb, slots, counts, first, lk, lx, ln, w2, vals, *refs):
    groups, (hg, cot, cw, sems) = split(refs, counts)
    copies = load(groups, cot, sems)
    hg[...] = jnp.zeros_like(hg)
    for copy in copies:
        copy.wait()
    project(cot, w2, cw)
    back_rows(nb, slots, first, lk, lx, ln, vals, cw, hg)


def lists_kernel(nb, slots, blank, *refs):
    cols_own, used_own, cols_far, used_far, v_hbm, lk, lx, ln, v_own, sem = refs
    bring = pltpu.make_async_copy(v_hbm, v_own, sem)
    bring.start()
    cols = ((cols_own, used_own), (cols_far, used_far))
    dom = lax.axis_index("dom")
    base = lax.axis_index("col") * slots
    stride = slots + GROUP
    for r in range(2 * nb):
        names, used = cols[r // nb]
        limit = used[r % nb]
        n = jnp.int32(0)
        for k in range(slots):
            block = names[r % nb, base + k]
            rel = lax.div(block, jnp.int32(nb)) ^ dom
            lk[r * stride + n] = k
            lx[r * stride + n] = (rel >> 1) * nb + lax.rem(block, jnp.int32(nb))
            ok = jnp.logical_and(base + k < limit, (rel & 1) == 0)
            n = n + ok.astype(jnp.int32)
        ln[r] = n
        for t in range(GROUP):
            lk[r * stride + n + t] = 0
            lx[r * stride + n + t] = blank
    bring.wait()


def put(ref, rows, value, narrow):
    width = value.shape[1]
    if narrow % LANES:
        ref[rows, :] = value.astype(ref.dtype)
        return
    col = lax.axis_index("col")
    for q in range(width // narrow):
        at = pl.ds(pl.multiple_of((col ^ q) * narrow, LANES), narrow)
        ref[rows, at] = value[:, q * narrow : (q + 1) * narrow].astype(ref.dtype)


def rows_product(nb, slots, r, lk, lx, ln, vals, source, width):
    base = r * (slots + GROUP)

    def step(g, acc):
        at = base + g * GROUP
        right = jnp.concatenate(
            [source[place(lx, at + t), :] for t in range(GROUP)], axis=0
        )
        return acc + jnp.dot(
            tiles(vals, r % nb, lk, at), right, preferred_element_type=F32
        )

    steps = (ln[r] + GROUP - 1) // GROUP
    return lax.fori_loop(0, steps, step, jnp.zeros((BLK, width), F32))


def first_kernel(nb, slots, counts, narrow, lk, lx, ln, v_own, v_far, *refs):
    groups, (keep, send, src, sems) = split(refs, counts)
    copies = load(groups, src, sems)
    width = src.shape[1]
    src[src.shape[0] - BLK :, :] = jnp.zeros((BLK, width), BF16)
    for copy in copies:
        copy.wait()
    for r in range(2 * nb):
        acc = rows_product(nb, slots, r, lk, lx, ln, v_own if r < nb else v_far, src, width)
        put(keep if r < nb else send, pl.ds(r % nb * BLK, BLK), acc, narrow)


def second_kernel(nb, slots, counts, narrow, lk, lx, ln, w1, w2, v_own, v_far, hg, hg_far, *refs):
    groups, (keep, send, gkeep, gsend, agg, hid, cot, mix, total, sems) = split(refs, counts)
    copies = load(groups[:-2], agg, sems)
    more = load(groups[-2:], cot, sems, len(copies))
    blocks, width = agg.shape
    chunk = nb * BLK
    hid[blocks:, :] = jnp.zeros((BLK, width), BF16)
    for copy in copies:
        copy.wait()
    total[...] = jnp.zeros_like(total)
    for g in range(blocks // chunk):
        rows = pl.ds(g * chunk, chunk)
        a = agg[rows, :]
        first = jnp.dot(a, w1[...], preferred_element_type=F32)
        sig = 0.5 * jnp.tanh(0.5 * first) + 0.5
        act = first * sig
        hid[rows, :] = act.astype(BF16)
        slope = sig + act * (1.0 - sig)
        grad = ((hg[rows, :] + hg_far[rows, :]) * slope).astype(BF16)
        total[...] += lax.dot_general(
            a, grad, (((0,), (0,)), ((), ())), preferred_element_type=F32
        )
    for r in range(2 * nb):
        acc = rows_product(nb, slots, r, lk, lx, ln, v_own if r < nb else v_far, hid, width)
        mix[r * BLK : (r + 1) * BLK, :] = acc.astype(BF16)
    for copy in more:
        copy.wait()
    core = lax.axis_index("dom") & 1
    everything = pl.ds(0, width)
    second = lax.dot_general(
        mix[...], cot[...], (((0,), (0,)), ((), ())), preferred_element_type=F32
    )

    @pl.when(core == 0)
    def _():
        put(gkeep, everything, total[...], narrow)
        put(gsend, everything, second, narrow)

    @pl.when(core == 1)
    def _():
        put(gkeep, everything, second, narrow)
        put(gsend, everything, total[...], narrow)

    for half, ref in enumerate((keep, send)):
        mine = mix[half * chunk : (half + 1) * chunk, :]
        value = jnp.dot(mine, w2[...], preferred_element_type=F32)
        put(ref, pl.ds(0, chunk), value, narrow)


def last_kernel(mine, other, grad_first, grad_second):
    core = lax.axis_index("dom") & 1

    @pl.when(core == 0)
    def _():
        grad_first[...] = mine[...]
        grad_second[...] = other[...]

    @pl.when(core == 1)
    def _():
        grad_first[...] = other[...]
        grad_second[...] = mine[...]


def any_spec():
    return pl.BlockSpec(memory_space=pl.ANY)


def vmem():
    return pl.BlockSpec(memory_space=pltpu.VMEM)


def smem():
    return pl.BlockSpec(memory_space=pltpu.SMEM)


def in_hbm(value):
    return pltpu.with_memory_space_constraint(value, pltpu.HBM)


def call(kernel, out, out_specs, in_specs, scratch, args, flops, grant=16):
    return pl.pallas_call(
        kernel,
        out_shape=tuple(jax.ShapeDtypeStruct(*o) for o in out),
        in_specs=in_specs,
        out_specs=tuple(out_specs),
        scratch_shapes=scratch,
        compiler_params=pltpu.CompilerParams(vmem_limit_bytes=grant << 20),
        cost_estimate=pl.CostEstimate(
            flops=flops, bytes_accessed=4 << 20, transcendentals=0
        ),
    )(*args)


def work(feats, w_first, w_second, block_cols, block_count, block_vals, cotangent):
    nd, nc = lax.axis_size("dom"), lax.axis_size("col")
    col = lax.axis_index("col")
    rows, narrow = feats.shape
    nb, slots = block_vals.shape[:2]
    width = narrow * nc
    blocks = nd // 2 * rows
    lists = 2 * nb * (slots + GROUP)
    dense = 2 * 2 * nb * slots * BLK * BLK * width // 2

    pieces = 1 if narrow % LANES else nc
    chunks = gather(widen(feats), pieces)
    cot_own = [widen(cotangent)]
    for cx in range(1, pieces):
        cot_own.append(swap(cotangent, "col", cx))
    v_far = swap(block_vals, "dom", 1)
    cols = (
        block_cols, block_count, swap(block_cols, "dom", 1), swap(block_count, "dom", 1)
    )
    cot_far = [swap(piece, "dom", 1) for piece in cot_own]

    lk, lx, ln, v_own = call(
        functools.partial(lists_kernel, nb, slots, blocks // BLK),
        [
            ((lists,), jnp.int32),
            ((lists,), jnp.int32),
            ((2 * nb,), jnp.int32),
            (block_vals.shape, BF16),
        ],
        [smem()] * 3 + [vmem()],
        [smem()] * 4 + [any_spec()],
        [pltpu.SemaphoreType.DMA],
        (*cols, in_hbm(block_vals)),
        1 << 20,
    )

    counts = tuple(len(g) for g in chunks)
    if pieces > 1:
        chunks[0][0] = in_hbm(feats)
    keep, send = call(
        functools.partial(first_kernel, nb, slots, counts, narrow),
        [((rows, width), F32), ((rows, width), BF16)],
        [vmem()] * 2,
        [smem()] * 3 + [vmem()] * 2 + [any_spec()] * sum(counts),
        [
            pltpu.VMEM((blocks + BLK, width), BF16),
            pltpu.SemaphoreType.DMA((sum(counts),)),
        ],
        (lk, lx, ln, v_own, v_far, *[p for g in chunks for p in g]),
        dense,
    )

    def back(first, vals, pieces):
        n = len(pieces)
        return call(
            functools.partial(back_kernel, nb, slots, (n,), first),
            [((blocks + BLK, width), F32)],
            [vmem()],
            [smem()] * 3 + [vmem()] * 2 + [any_spec()] * n,
            [
                pltpu.VMEM((rows, width), BF16),
                pltpu.VMEM((rows, width), BF16),
                pltpu.SemaphoreType.DMA((n,)),
            ],
            (lk, lx, ln, w_second, vals, *pieces),
            dense // 2,
        )[0]

    hg = back(0, v_own, cot_own)
    hg_far = back(nb, v_far, cot_far)

    def feature(value, cx):
        axis = value.ndim - 1
        if narrow % LANES:
            at = (col ^ cx) * narrow
            return lax.dynamic_slice_in_dim(value, at, narrow, axis)
        return lax.slice_in_dim(value, cx * narrow, (cx + 1) * narrow, axis=axis)

    def reduce_rows(keep, send):
        part = keep + swap(send, "dom", 1).astype(F32)
        total = feature(part, 0)
        for cx in range(1, nc):
            piece = feature(part, cx).astype(BF16)
            total = total + swap(piece, "col", cx).astype(F32)
        return total

    agg = reduce_rows(keep, send).astype(BF16)

    chunks = gather(widen(agg), pieces)
    groups = chunks + [cot_own, cot_far]
    counts = tuple(len(g) for g in groups)
    keep, send, gkeep, gsend = call(
        functools.partial(second_kernel, nb, slots, counts, narrow),
        [
            ((rows, width), F32),
            ((rows, width), BF16),
            ((width, width), F32),
            ((width, width), BF16),
        ],
        [vmem()] * 4,
        [smem()] * 3 + [vmem()] * 6 + [any_spec()] * sum(counts),
        [
            pltpu.VMEM((blocks, width), BF16),
            pltpu.VMEM((blocks + BLK, width), BF16),
            pltpu.VMEM((2 * rows, width), BF16),
            pltpu.VMEM((2 * rows, width), BF16),
            pltpu.VMEM((width, width), F32),
            pltpu.SemaphoreType.DMA((sum(counts),)),
        ],
        (lk, lx, ln, w_first, w_second, v_own, v_far, hg, hg_far)
        + tuple(p for g in groups for p in g),
        4 * dense,
    )

    part = gkeep + swap(gsend, "dom", 1).astype(F32)
    mine = feature(part, 0)
    for cx in range(1, nc):
        piece = swap(feature(part, cx).astype(BF16), "col", cx)
        mine = mine + piece.astype(F32)
    bit = 2
    while bit < nd:
        half = mine.astype(BF16)
        mine = half.astype(F32) + swap(half, "dom", bit).astype(F32)
        bit *= 2
    other = swap(mine, "dom", 1)
    grad_first, grad_second = call(
        last_kernel,
        [((width, narrow), F32)] * 2,
        [vmem()] * 2,
        [vmem()] * 2,
        [],
        (mine, other),
        width * narrow,
    )
    output = reduce_rows(keep, send)
    return output, grad_first, grad_second


def solution(mesh):
    in_specs = (
        P("dom", "col"),
        P(),
        P(),
        P("dom", None),
        P("dom"),
        P("dom", "col", None, None),
        P("dom", "col"),
    )
    out_specs = (P("dom", "col"), P(None, "col"), P(None, "col"))
    return jax.shard_map(work, mesh=mesh, in_specs=in_specs, out_specs=out_specs, check_vma=False)
```

```python
import functools

import jax
import jax.numpy as jnp
from jax import lax
from jax.experimental import pallas as pl
from jax.experimental.pallas import tpu as pltpu
from jax.sharding import PartitionSpec as P


BLK = 128
GROUP = 8
BACK = 4
PART = 512
LANES = 128
F32 = jnp.float32
BF16 = jnp.bfloat16


def swap(value, axis, mask):
    size = lax.axis_size(axis)
    return lax.ppermute(value, axis, [(i, i ^ mask) for i in range(size)])


def widen(own):
    if own.shape[1] % LANES:
        return lax.all_gather(own, "col", axis=1, tiled=True)
    return own


def gather_order(nd, nc):
    far = list(range(4, nd, 4))
    order = [(v, 0, (0, 0), "dom") for v in far[:2]]
    late = [(v, 0, (0, 0), "dom") for v in far[2:]]
    corners = []
    for n, v in enumerate((0, *far)):
        if nd >= 4:
            order.append((v | 2, 0, (v, 0), "dom"))
        order += [(v, cx, (v, 0), "col") for cx in range(1, nc)]
        order += late + corners
        late, corners = [], []
        for cx in range(1, nc):
            if nd >= 4 and (n + cx) % 2:
                corners.append((v | 2, cx, (v, cx), "dom"))
            elif nd >= 4:
                corners.append((v | 2, cx, (v | 2, 0), "col"))
    return order + corners


def gather(own, nc):
    nd = lax.axis_size("dom")
    got = {(0, 0): own}
    for v, cx, (sv, sc), axis in gather_order(nd, nc):
        mask = v ^ sv if axis == "dom" else cx ^ sc
        got[v, cx] = swap(got[sv, sc], axis, mask)
    return [[got[v, cx] for cx in range(nc)] for v in range(0, nd, 2)]


def load(groups, dest, sems, first=0):
    copies = []
    col = lax.axis_index("col")
    for g, pieces in enumerate(groups):
        for cx, piece in enumerate(pieces):
            rows, wide = piece.shape
            lane = 0
            if len(pieces) > 1:
                lane = pl.multiple_of((col ^ cx) * wide, LANES)
            copies.append(
                pltpu.make_async_copy(
                    piece,
                    dest.at[pl.ds(g * rows, rows), pl.ds(lane, wide)],
                    sems.at[first + len(copies)],
                )
            )
    for copy in copies:
        copy.start()
    return copies


def split(refs, counts):
    out, at = [], 0
    for n in counts:
        out.append(refs[at : at + n])
        at += n
    return out, refs[at:]


class Part:
    def __init__(self, ref, start):
        self.ref, self.start = ref, start

    def __getitem__(self, i):
        return self.ref[self.start + i]

    def __setitem__(self, i, value):
        self.ref[self.start + i] = value


def plan_size(nb, slots):
    return 2 * nb * (2 * (slots + GROUP) + 1)


def plan_parts(plan, nb, slots):
    size = 2 * nb * (slots + GROUP)
    return Part(plan, 0), Part(plan, size), Part(plan, 2 * size)


def tiles(vals, r, lk, at, count):
    return jnp.concatenate([vals[r, lk[at + t]] for t in range(count)], axis=1)


def place(lx, at):
    return pl.ds(pl.multiple_of(lx[at] * BLK, BLK), BLK)


def row_of(i, size):
    return pl.ds(pl.multiple_of(i * size, size), size)


def back_rows(nb, slots, first, lk, lx, ln, vals, cw, hg):
    def row(i, carry):
        grad = cw[row_of(i, BLK), :]
        base = (first + i) * (slots + GROUP)

        def step(g, carry):
            at = base + g * BACK
            prod = lax.dot_general(
                tiles(vals, i, lk, at, BACK),
                grad,
                (((0,), (0,)), ((), ())),
                preferred_element_type=F32,
            )
            for t in range(BACK):
                hg[place(lx, at + t), :] += prod[t * BLK : (t + 1) * BLK, :]
            return carry

        return lax.fori_loop(0, (ln[first + i] + BACK - 1) // BACK, step, carry)

    lax.fori_loop(0, nb, row, 0)


def project(cot, w2, cw):
    cw[...] = lax.dot_general(
        cot[...], w2[...], (((1,), (1,)), ((), ())), preferred_element_type=F32
    ).astype(BF16)


def back_kernel(nb, slots, counts, first, plan, w2, vals, *refs):
    groups, (hg, cot, cw, sems) = split(refs, counts)
    lk, lx, ln = plan_parts(plan, nb, slots)
    copies = load(groups, cot, sems)
    hg[...] = jnp.zeros_like(hg)
    for copy in copies:
        copy.wait()
    project(cot, w2, cw)
    back_rows(nb, slots, first, lk, lx, ln, vals, cw, hg)


def lists_kernel(nb, slots, blank, *refs):
    v_hbm, plan, v_own, cols_own, used_own, cols_far, used_far, sem = refs[4:]
    lk, lx, ln = plan_parts(plan, nb, slots)
    held = (cols_own, used_own, cols_far, used_far)
    scalars = [
        pltpu.make_async_copy(ref, here, sem.at[1 + n])
        for n, (ref, here) in enumerate(zip(refs[:4], held))
    ]
    for copy in scalars:
        copy.start()
    bring = pltpu.make_async_copy(v_hbm, v_own, sem.at[0])
    bring.start()
    for copy in scalars:
        copy.wait()
    dom = lax.axis_index("dom")
    base = lax.axis_index("col") * slots
    stride = slots + GROUP
    bits = nb.bit_length() - 1
    halves = ((cols_own, used_own), (cols_far, used_far))
    for half, (names, used) in enumerate(halves):

        def row(i, carry, half=half, names=names, used=used):
            start = (half * nb + i) * stride
            limit = used[i] - base
            n = start
            for k in range(slots):
                block = names[i, base + k]
                if nb == 1 << bits:
                    rel = block ^ (dom << bits)
                    ok = (rel & nb) == 0
                    spot = ((rel >> (bits + 1)) << bits) | (rel & (nb - 1))
                else:
                    rel = lax.div(block, jnp.int32(nb)) ^ dom
                    ok = (rel & 1) == 0
                    spot = (rel >> 1) * nb + lax.rem(block, jnp.int32(nb))
                lk[n] = k
                lx[n] = spot
                n = n + jnp.logical_and(k < limit, ok).astype(jnp.int32)
            ln[half * nb + i] = n - start
            for t in range(GROUP):
                lk[n + t] = 0
                lx[n + t] = blank
            return carry

        lax.fori_loop(0, nb, row, 0)
    bring.wait()


def put(ref, rows, value, narrow):
    width = value.shape[1]
    if narrow % LANES:
        ref[rows, :] = value.astype(ref.dtype)
        return
    col = lax.axis_index("col")
    for q in range(width // narrow):
        at = pl.ds(pl.multiple_of((col ^ q) * narrow, LANES), narrow)
        ref[rows, at] = value[:, q * narrow : (q + 1) * narrow].astype(ref.dtype)


def rows_product(slots, r, i, lk, lx, ln, vals, source, width):
    base = r * (slots + GROUP)

    def step(g, acc):
        at = base + g * GROUP
        right = jnp.concatenate(
            [source[place(lx, at + t), :] for t in range(GROUP)], axis=0
        )
        return acc + jnp.dot(
            tiles(vals, i, lk, at, GROUP), right, preferred_element_type=F32
        )

    steps = (ln[r] + GROUP - 1) // GROUP
    return lax.fori_loop(0, steps, step, jnp.zeros((BLK, width), F32))


def first_kernel(nb, slots, counts, narrow, plan, v_own, v_far, *refs):
    groups, (keep, send, src, sems) = split(refs, counts)
    lk, lx, ln = plan_parts(plan, nb, slots)
    copies = load(groups, src, sems)
    width = src.shape[1]
    src[src.shape[0] - BLK :, :] = jnp.zeros((BLK, width), BF16)
    for copy in copies:
        copy.wait()
    for half, (vals, ref) in enumerate(((v_own, keep), (v_far, send))):

        def row(i, carry, half=half, vals=vals, ref=ref):
            r = half * nb + i
            acc = rows_product(slots, r, i, lk, lx, ln, vals, src, width)
            put(ref, row_of(i, BLK), acc, narrow)
            return carry

        lax.fori_loop(0, nb, row, 0)


def second_kernel(
    nb, slots, counts, narrow, plan, w1, w2, v_own, v_far, hg, hg_far, *refs
):
    lk, lx, ln = plan_parts(plan, nb, slots)
    groups, (keep, send, gkeep, gsend, agg, hid, cot, mix, total, sems) = split(refs, counts)
    copies = load(groups[:-2], agg, sems)
    more = load(groups[-2:], cot, sems, len(copies))
    blocks, width = agg.shape
    chunk = nb * BLK
    hid[blocks:, :] = jnp.zeros((BLK, width), BF16)
    for copy in copies:
        copy.wait()
    total[...] = jnp.zeros_like(total)

    for g in range(blocks // PART):
        rows = pl.ds(g * PART, PART)
        a = agg[rows, :]
        first = jnp.dot(a, w1[...], preferred_element_type=F32)
        sig = 0.5 * jnp.tanh(0.5 * first) + 0.5
        act = first * sig
        hid[rows, :] = act.astype(BF16)
        slope = sig + act * (1.0 - sig)
        grad = ((hg[rows, :] + hg_far[rows, :]) * slope).astype(BF16)
        total[...] += lax.dot_general(
            a, grad, (((0,), (0,)), ((), ())), preferred_element_type=F32
        )
    for half, vals in enumerate((v_own, v_far)):

        def row(i, carry, half=half, vals=vals):
            r = half * nb + i
            acc = rows_product(slots, r, i, lk, lx, ln, vals, hid, width)
            mix[row_of(r, BLK), :] = acc.astype(BF16)
            return carry

        lax.fori_loop(0, nb, row, 0)
    for copy in more:
        copy.wait()
    core = lax.axis_index("dom") & 1
    everything = pl.ds(0, width)
    second = lax.dot_general(
        mix[...], cot[...], (((0,), (0,)), ((), ())), preferred_element_type=F32
    )

    @pl.when(core == 0)
    def _():
        put(gkeep, everything, total[...], narrow)
        put(gsend, everything, second, narrow)

    @pl.when(core == 1)
    def _():
        put(gkeep, everything, second, narrow)
        put(gsend, everything, total[...], narrow)

    for half, ref in enumerate((keep, send)):
        mine = mix[half * chunk : (half + 1) * chunk, :]
        value = jnp.dot(mine, w2[...], preferred_element_type=F32)
        put(ref, pl.ds(0, chunk), value, narrow)


def last_kernel(mine, other, grad_first, grad_second):
    core = lax.axis_index("dom") & 1

    @pl.when(core == 0)
    def _():
        grad_first[...] = mine[...]
        grad_second[...] = other[...]

    @pl.when(core == 1)
    def _():
        grad_first[...] = other[...]
        grad_second[...] = mine[...]


def any_spec():
    return pl.BlockSpec(memory_space=pl.ANY)


def vmem():
    return pl.BlockSpec(memory_space=pltpu.VMEM)


def smem():
    return pl.BlockSpec(memory_space=pltpu.SMEM)


def in_hbm(value):
    return pltpu.with_memory_space_constraint(value, pltpu.HBM)


def call(kernel, out, out_specs, in_specs, scratch, args, flops, grant=16):
    return pl.pallas_call(
        kernel,
        out_shape=tuple(jax.ShapeDtypeStruct(*o) for o in out),
        in_specs=in_specs,
        out_specs=tuple(out_specs),
        scratch_shapes=scratch,
        compiler_params=pltpu.CompilerParams(vmem_limit_bytes=grant << 20),
        cost_estimate=pl.CostEstimate(
            flops=flops, bytes_accessed=4 << 20, transcendentals=0
        ),
    )(*args)


def work(feats, w_first, w_second, block_cols, block_count, block_vals, cotangent):
    nd, nc = lax.axis_size("dom"), lax.axis_size("col")
    col = lax.axis_index("col")
    rows, narrow = feats.shape
    nb, slots = block_vals.shape[:2]
    width = narrow * nc
    blocks = nd // 2 * rows
    dense = 2 * 2 * nb * slots * BLK * BLK * width // 2

    pieces = 1 if narrow % LANES else nc
    chunks = gather(widen(feats), pieces)
    cot_own = [widen(cotangent)]
    for cx in range(1, pieces):
        cot_own.append(swap(cotangent, "col", cx))
    v_far = swap(block_vals, "dom", 1)
    cols = (
        block_cols, block_count, swap(block_cols, "dom", 1), swap(block_count, "dom", 1)
    )
    cot_far = [swap(piece, "dom", 1) for piece in cot_own]

    plan, v_own = call(
        functools.partial(lists_kernel, nb, slots, blocks // BLK),
        [
            ((plan_size(nb, slots),), jnp.int32),
            (block_vals.shape, BF16),
        ],
        [smem(), vmem()],
        [any_spec()] * 5,
        [
            pltpu.SMEM(block_cols.shape, jnp.int32),
            pltpu.SMEM(block_count.shape, jnp.int32),
            pltpu.SMEM(block_cols.shape, jnp.int32),
            pltpu.SMEM(block_count.shape, jnp.int32),
            pltpu.SemaphoreType.DMA((5,)),
        ],
        (*[in_hbm(c) for c in cols[:2]], *cols[2:], in_hbm(block_vals)),
        1 << 20,
    )

    counts = tuple(len(g) for g in chunks)
    if pieces > 1:
        chunks[0][0] = in_hbm(feats)
    keep, send = call(
        functools.partial(first_kernel, nb, slots, counts, narrow),
        [((rows, width), F32), ((rows, width), BF16)],
        [vmem()] * 2,
        [smem()] + [vmem()] * 2 + [any_spec()] * sum(counts),
        [
            pltpu.VMEM((blocks + BLK, width), BF16),
            pltpu.SemaphoreType.DMA((sum(counts),)),
        ],
        (plan, v_own, v_far, *[p for g in chunks for p in g]),
        dense,
    )

    def back(first, vals, pieces):
        n = len(pieces)
        return call(
            functools.partial(back_kernel, nb, slots, (n,), first),
            [((blocks + BLK, width), F32)],
            [vmem()],
            [smem()] + [vmem()] * 2 + [any_spec()] * n,
            [
                pltpu.VMEM((rows, width), BF16),
                pltpu.VMEM((rows, width), BF16),
                pltpu.SemaphoreType.DMA((n,)),
            ],
            (plan, w_second, vals, *pieces),
            dense // 2,
        )[0]

    hg = back(0, v_own, cot_own)
    hg_far = back(nb, v_far, cot_far)

    def feature(value, cx):
        axis = value.ndim - 1
        if narrow % LANES:
            at = (col ^ cx) * narrow
            return lax.dynamic_slice_in_dim(value, at, narrow, axis)
        return lax.slice_in_dim(value, cx * narrow, (cx + 1) * narrow, axis=axis)

    def reduce_rows(keep, send):
        part = keep + swap(send, "dom", 1).astype(F32)
        total = feature(part, 0)
        for cx in range(1, nc):
            piece = feature(part, cx).astype(BF16)
            total = total + swap(piece, "col", cx).astype(F32)
        return total

    agg = reduce_rows(keep, send).astype(BF16)

    chunks = gather(widen(agg), pieces)
    groups = chunks + [cot_own, cot_far]
    counts = tuple(len(g) for g in groups)
    keep, send, gkeep, gsend = call(
        functools.partial(second_kernel, nb, slots, counts, narrow),
        [
            ((rows, width), F32),
            ((rows, width), BF16),
            ((width, width), F32),
            ((width, width), BF16),
        ],
        [vmem()] * 4,
        [smem()] + [vmem()] * 6 + [any_spec()] * sum(counts),
        [
            pltpu.VMEM((blocks, width), BF16),
            pltpu.VMEM((blocks + BLK, width), BF16),
            pltpu.VMEM((2 * rows, width), BF16),
            pltpu.VMEM((2 * rows, width), BF16),
            pltpu.VMEM((width, width), F32),
            pltpu.SemaphoreType.DMA((sum(counts),)),
        ],
        (plan, w_first, w_second, v_own, v_far, hg, hg_far)
        + tuple(p for g in groups for p in g),
        4 * dense,
    )

    part = gkeep + swap(gsend, "dom", 1).astype(F32)
    mine = feature(part, 0)
    for cx in range(1, nc):
        piece = swap(feature(part, cx).astype(BF16), "col", cx)
        mine = mine + piece.astype(F32)
    bit = 2
    while bit < nd:
        half = mine.astype(BF16)
        mine = half.astype(F32) + swap(half, "dom", bit).astype(F32)
        bit *= 2
    other = swap(mine, "dom", 1)
    grad_first, grad_second = call(
        last_kernel,
        [((width, narrow), F32)] * 2,
        [vmem()] * 2,
        [vmem()] * 2,
        [],
        (mine, other),
        width * narrow,
    )
    output = reduce_rows(keep, send)
    return output, grad_first, grad_second


def solution(mesh):
    in_specs = (
        P("dom", "col"),
        P(),
        P(),
        P("dom", None),
        P("dom"),
        P("dom", "col", None, None),
        P("dom", "col"),
    )
    out_specs = (P("dom", "col"), P(None, "col"), P(None, "col"))
    return jax.shard_map(work, mesh=mesh, in_specs=in_specs, out_specs=out_specs, check_vma=False)
```

```python
import functools

import jax
import jax.numpy as jnp
from jax import lax
from jax.experimental import pallas as pl
from jax.experimental.pallas import tpu as pltpu
from jax.sharding import PartitionSpec as P


BLK = 128
GROUP = 12
BACK = 4
PART = 512
LANES = 128
F32 = jnp.float32
BF16 = jnp.bfloat16


def swap(value, axis, mask):
    size = lax.axis_size(axis)
    return lax.ppermute(value, axis, [(i, i ^ mask) for i in range(size)])


def widen(own):
    if own.shape[1] % LANES:
        return lax.all_gather(own, "col", axis=1, tiled=True)
    return own


def gather_order(nd, nc):
    far = list(range(4, nd, 4))
    order = [(v, 0, (0, 0), "dom") for v in far[:2]]
    late = [(v, 0, (0, 0), "dom") for v in far[2:]]
    corners = []
    for n, v in enumerate((0, *far)):
        if nd >= 4:
            order.append((v | 2, 0, (v, 0), "dom"))
        order += [(v, cx, (v, 0), "col") for cx in range(1, nc)]
        order += late + corners
        late, corners = [], []
        for cx in range(1, nc):
            if nd >= 4 and (n + cx) % 2:
                corners.append((v | 2, cx, (v, cx), "dom"))
            elif nd >= 4:
                corners.append((v | 2, cx, (v | 2, 0), "col"))
    return order + corners


def gather(own, nc):
    nd = lax.axis_size("dom")
    got = {(0, 0): own}
    for v, cx, (sv, sc), axis in gather_order(nd, nc):
        mask = v ^ sv if axis == "dom" else cx ^ sc
        got[v, cx] = swap(got[sv, sc], axis, mask)
    return [[got[v, cx] for cx in range(nc)] for v in range(0, nd, 2)]


def load(groups, dest, sems, first=0):
    copies = []
    col = lax.axis_index("col")
    for g, pieces in enumerate(groups):
        for cx, piece in enumerate(pieces):
            rows, wide = piece.shape
            lane = 0
            if len(pieces) > 1:
                lane = pl.multiple_of((col ^ cx) * wide, LANES)
            copies.append(
                pltpu.make_async_copy(
                    piece,
                    dest.at[pl.ds(g * rows, rows), pl.ds(lane, wide)],
                    sems.at[first + len(copies)],
                )
            )
    for copy in copies:
        copy.start()
    return copies


def split(refs, counts):
    out, at = [], 0
    for n in counts:
        out.append(refs[at : at + n])
        at += n
    return out, refs[at:]


class Part:
    def __init__(self, ref, start):
        self.ref, self.start = ref, start

    def __getitem__(self, i):
        return self.ref[self.start + i]

    def __setitem__(self, i, value):
        self.ref[self.start + i] = value


def plan_size(nb, slots):
    return 2 * nb * (2 * (slots + GROUP) + 1)


def plan_parts(plan, nb, slots):
    size = 2 * nb * (slots + GROUP)
    return Part(plan, 0), Part(plan, size), Part(plan, 2 * size)


def tiles(vals, r, lk, at, count):
    return jnp.concatenate([vals[r, lk[at + t]] for t in range(count)], axis=1)


def place(lx, at):
    return pl.ds(pl.multiple_of(lx[at] * BLK, BLK), BLK)


def row_of(i, size):
    return pl.ds(pl.multiple_of(i * size, size), size)


def back_rows(nb, slots, first, lk, lx, ln, vals, cw, hg):
    def row(i, carry):
        grad = cw[row_of(i, BLK), :]
        base = (first + i) * (slots + GROUP)

        def step(g, carry):
            at = base + g * BACK
            prod = lax.dot_general(
                tiles(vals, i, lk, at, BACK),
                grad,
                (((0,), (0,)), ((), ())),
                preferred_element_type=F32,
            )
            for t in range(BACK):
                hg[place(lx, at + t), :] += prod[t * BLK : (t + 1) * BLK, :]
            return carry

        return lax.fori_loop(0, (ln[first + i] + BACK - 1) // BACK, step, carry)

    lax.fori_loop(0, nb, row, 0)


def project(cot, w2, cw):
    cw[...] = lax.dot_general(
        cot[...], w2[...], (((1,), (1,)), ((), ())), preferred_element_type=F32
    ).astype(BF16)


def back_kernel(nb, slots, counts, first, plan, w2, vals, *refs):
    groups, (hg, cot, cw, sems) = split(refs, counts)
    lk, lx, ln = plan_parts(plan, nb, slots)
    copies = load(groups, cot, sems)
    hg[...] = jnp.zeros_like(hg)
    for copy in copies:
        copy.wait()
    project(cot, w2, cw)
    back_rows(nb, slots, first, lk, lx, ln, vals, cw, hg)


def lists_kernel(nb, slots, blank, *refs):
    v_hbm, plan, v_own, cols_own, used_own, cols_far, used_far, sem = refs[4:]
    lk, lx, ln = plan_parts(plan, nb, slots)
    held = (cols_own, used_own, cols_far, used_far)
    scalars = [
        pltpu.make_async_copy(ref, here, sem.at[1 + n])
        for n, (ref, here) in enumerate(zip(refs[:4], held))
    ]
    for copy in scalars:
        copy.start()
    bring = pltpu.make_async_copy(v_hbm, v_own, sem.at[0])
    bring.start()
    for copy in scalars:
        copy.wait()
    dom = lax.axis_index("dom")
    base = lax.axis_index("col") * slots
    stride = slots + GROUP
    bits = nb.bit_length() - 1
    halves = ((cols_own, used_own), (cols_far, used_far))
    for half, (names, used) in enumerate(halves):

        def row(i, carry, half=half, names=names, used=used):
            start = (half * nb + i) * stride
            limit = used[i] - base
            n = start
            for k in range(slots):
                block = names[i, base + k]
                if nb == 1 << bits:
                    rel = block ^ (dom << bits)
                    ok = (rel & nb) == 0
                    spot = ((rel >> (bits + 1)) << bits) | (rel & (nb - 1))
                else:
                    rel = lax.div(block, jnp.int32(nb)) ^ dom
                    ok = (rel & 1) == 0
                    spot = (rel >> 1) * nb + lax.rem(block, jnp.int32(nb))
                lk[n] = k
                lx[n] = spot
                n = n + jnp.logical_and(k < limit, ok).astype(jnp.int32)
            ln[half * nb + i] = n - start
            for t in range(GROUP):
                lk[n + t] = 0
                lx[n + t] = blank
            return carry

        lax.fori_loop(0, nb, row, 0)
    bring.wait()


def put(ref, rows, value, narrow):
    width = value.shape[1]
    if narrow % LANES:
        ref[rows, :] = value.astype(ref.dtype)
        return
    col = lax.axis_index("col")
    for q in range(width // narrow):
        at = pl.ds(pl.multiple_of((col ^ q) * narrow, LANES), narrow)
        ref[rows, at] = value[:, q * narrow : (q + 1) * narrow].astype(ref.dtype)


def rows_product(slots, r, i, lk, lx, ln, vals, source, width):
    base = r * (slots + GROUP)

    def step(g, acc):
        at = base + g * GROUP
        right = jnp.concatenate(
            [source[place(lx, at + t), :] for t in range(GROUP)], axis=0
        )
        return acc + jnp.dot(
            tiles(vals, i, lk, at, GROUP), right, preferred_element_type=F32
        )

    steps = (ln[r] + GROUP - 1) // GROUP
    return lax.fori_loop(0, steps, step, jnp.zeros((BLK, width), F32))


def times_rows(nb, slots, first, plan, vals, source, ref, narrow):
    lk, lx, ln = plan_parts(plan, nb, slots)

    def row(i, carry):
        acc = rows_product(slots, first + i, i, lk, lx, ln, vals, source, source.shape[1])
        put(ref, row_of(i, BLK), acc, narrow)
        return carry

    lax.fori_loop(0, nb, row, 0)


def first_far_kernel(nb, slots, counts, narrow, plan, vals, *refs):
    groups, (src, send, sems) = split(refs, counts)
    copies = load(groups, src, sems)
    src[src.shape[0] - BLK :, :] = jnp.zeros((BLK, src.shape[1]), BF16)
    for copy in copies:
        copy.wait()
    times_rows(nb, slots, nb, plan, vals, src, send, narrow)


def first_own_kernel(nb, slots, narrow, plan, vals, src, keep):
    times_rows(nb, slots, 0, plan, vals, src, keep, narrow)


def activate(agg, w1, hg, hg_far, hid, total, places):
    for g in range(agg.shape[0] // PART):
        rows = pl.ds(g * PART, PART)
        there = pl.ds(places + g * PART, PART)
        a = agg[rows, :]
        first = jnp.dot(a, w1[...], preferred_element_type=F32)
        sig = 0.5 * jnp.tanh(0.5 * first) + 0.5
        act = first * sig
        hid[there, :] = act.astype(BF16)
        slope = sig + act * (1.0 - sig)
        grad = ((hg[there, :] + hg_far[there, :]) * slope).astype(BF16)
        total[...] += lax.dot_general(
            a, grad, (((0,), (0,)), ((), ())), preferred_element_type=F32
        )


def half_kernel(counts, w1, hg, hg_far, *refs):
    groups, (hid, total, agg, sems) = split(refs, counts)
    copies = load(groups, agg, sems)
    total[...] = jnp.zeros_like(total)
    for copy in copies:
        copy.wait()
    activate(agg, w1, hg, hg_far, hid, total, 0)


def second_kernel(
    nb, slots, counts, narrow, plan, w1, v_own, v_far, hg, hg_far, half, *refs
):
    lk, lx, ln = plan_parts(plan, nb, slots)
    part, *refs = refs
    groups, (mix, gkeep, gsend, agg, hid, cot, total, sems) = split(
        refs, counts
    )
    copies = load(groups[:-2], agg, sems)
    more = load(groups[-2:], cot, sems, len(copies))
    done = half.shape[0]
    bring = pltpu.make_async_copy(
        half, hid.at[pl.ds(0, done), :], sems.at[sum(counts)]
    )
    bring.start()
    blocks, width = done + agg.shape[0], agg.shape[1]
    chunk = nb * BLK
    hid[blocks:, :] = jnp.zeros((BLK, width), BF16)
    total[...] = part[...]
    for copy in copies:
        copy.wait()
    activate(agg, w1, hg, hg_far, hid, total, done)
    bring.wait()
    for half, vals in enumerate((v_own, v_far)):

        def row(i, carry, half=half, vals=vals):
            r = half * nb + i
            acc = rows_product(slots, r, i, lk, lx, ln, vals, hid, width)
            mix[row_of(r, BLK), :] = acc.astype(BF16)
            return carry

        lax.fori_loop(0, nb, row, 0)
    for copy in more:
        copy.wait()
    core = lax.axis_index("dom") & 1
    everything = pl.ds(0, width)
    second = lax.dot_general(
        mix[...], cot[...], (((0,), (0,)), ((), ())), preferred_element_type=F32
    )

    @pl.when(core == 0)
    def _():
        put(gkeep, everything, total[...], narrow)
        put(gsend, everything, second, narrow)

    @pl.when(core == 1)
    def _():
        put(gkeep, everything, second, narrow)
        put(gsend, everything, total[...], narrow)


def out_kernel(narrow, mix, w2, keep, send):
    chunk = keep.shape[0]
    for half, ref in enumerate((keep, send)):
        mine = mix[half * chunk : (half + 1) * chunk, :]
        value = jnp.dot(mine, w2[...], preferred_element_type=F32)
        put(ref, pl.ds(0, chunk), value, narrow)


def last_kernel(mine, other, grad_first, grad_second):
    core = lax.axis_index("dom") & 1

    @pl.when(core == 0)
    def _():
        grad_first[...] = mine[...]
        grad_second[...] = other[...]

    @pl.when(core == 1)
    def _():
        grad_first[...] = other[...]
        grad_second[...] = mine[...]


def any_spec():
    return pl.BlockSpec(memory_space=pl.ANY)


def vmem():
    return pl.BlockSpec(memory_space=pltpu.VMEM)


def smem():
    return pl.BlockSpec(memory_space=pltpu.SMEM)


def in_hbm(value):
    return pltpu.with_memory_space_constraint(value, pltpu.HBM)


def call(kernel, out, out_specs, in_specs, scratch, args, flops, grant=16):
    return pl.pallas_call(
        kernel,
        out_shape=tuple(jax.ShapeDtypeStruct(*o) for o in out),
        in_specs=in_specs,
        out_specs=tuple(out_specs),
        scratch_shapes=scratch,
        compiler_params=pltpu.CompilerParams(vmem_limit_bytes=grant << 20),
        cost_estimate=pl.CostEstimate(
            flops=flops, bytes_accessed=4 << 20, transcendentals=0
        ),
    )(*args)


def work(feats, w_first, w_second, block_cols, block_count, block_vals, cotangent):
    nd, nc = lax.axis_size("dom"), lax.axis_size("col")
    col = lax.axis_index("col")
    rows, narrow = feats.shape
    nb, slots = block_vals.shape[:2]
    width = narrow * nc
    blocks = nd // 2 * rows
    dense = 2 * 2 * nb * slots * BLK * BLK * width // 2

    pieces = 1 if narrow % LANES else nc
    chunks = gather(widen(feats), pieces)
    cot_own = [widen(cotangent)]
    for cx in range(1, pieces):
        cot_own.append(swap(cotangent, "col", cx))
    v_far = swap(block_vals, "dom", 1)
    cols = (
        block_cols, block_count, swap(block_cols, "dom", 1), swap(block_count, "dom", 1)
    )
    cot_far = [swap(piece, "dom", 1) for piece in cot_own]

    plan, v_own = call(
        functools.partial(lists_kernel, nb, slots, blocks // BLK),
        [
            ((plan_size(nb, slots),), jnp.int32),
            (block_vals.shape, BF16),
        ],
        [smem(), vmem()],
        [any_spec()] * 5,
        [
            pltpu.SMEM(block_cols.shape, jnp.int32),
            pltpu.SMEM(block_count.shape, jnp.int32),
            pltpu.SMEM(block_cols.shape, jnp.int32),
            pltpu.SMEM(block_count.shape, jnp.int32),
            pltpu.SemaphoreType.DMA((5,)),
        ],
        (*[in_hbm(c) for c in cols[:2]], *cols[2:], in_hbm(block_vals)),
        1 << 20,
    )

    counts = tuple(len(g) for g in chunks)
    if pieces > 1:
        chunks[0][0] = in_hbm(feats)
    src, send = call(
        functools.partial(first_far_kernel, nb, slots, counts, narrow),
        [((blocks + BLK, width), BF16), ((rows, width), BF16)],
        [vmem()] * 2,
        [smem(), vmem()] + [any_spec()] * sum(counts),
        [pltpu.SemaphoreType.DMA((sum(counts),))],
        (plan, v_far, *[p for g in chunks for p in g]),
        dense // 2,
    )
    (keep,) = call(
        functools.partial(first_own_kernel, nb, slots, narrow),
        [((rows, width), F32)],
        [vmem()],
        [smem(), vmem(), vmem()],
        [],
        (plan, v_own, src),
        dense // 2,
    )

    def back(first, vals, pieces):
        n = len(pieces)
        return call(
            functools.partial(back_kernel, nb, slots, (n,), first),
            [((blocks + BLK, width), F32)],
            [vmem()],
            [smem()] + [vmem()] * 2 + [any_spec()] * n,
            [
                pltpu.VMEM((rows, width), BF16),
                pltpu.VMEM((rows, width), BF16),
                pltpu.SemaphoreType.DMA((n,)),
            ],
            (plan, w_second, vals, *pieces),
            dense // 2,
        )[0]

    hg = back(0, v_own, cot_own)
    hg_far = back(nb, v_far, cot_far)

    def feature(value, cx):
        axis = value.ndim - 1
        if narrow % LANES:
            at = (col ^ cx) * narrow
            return lax.dynamic_slice_in_dim(value, at, narrow, axis)
        return lax.slice_in_dim(value, cx * narrow, (cx + 1) * narrow, axis=axis)

    def reduce_rows(keep, send):
        part = keep + swap(send, "dom", 1).astype(F32)
        total = feature(part, 0)
        for cx in range(1, nc):
            piece = feature(part, cx).astype(BF16)
            total = total + swap(piece, "col", cx).astype(F32)
        return total

    agg = reduce_rows(keep, send).astype(BF16)

    chunks = gather(widen(agg), pieces)
    early = (len(chunks) + 1) // 2
    counts = tuple(len(g) for g in chunks[:early])
    half, total = call(
        functools.partial(half_kernel, counts),
        [((early * rows, width), BF16), ((width, width), F32)],
        [vmem()] * 2,
        [vmem()] * 3 + [any_spec()] * sum(counts),
        [
            pltpu.VMEM((early * rows, width), BF16),
            pltpu.SemaphoreType.DMA((sum(counts),)),
        ],
        (w_first, hg, hg_far, *[p for g in chunks[:early] for p in g]),
        dense,
    )
    groups = chunks[early:] + [cot_own, cot_far]
    counts = tuple(len(g) for g in groups)
    mix, gkeep, gsend = call(
        functools.partial(second_kernel, nb, slots, counts, narrow),
        [
            ((2 * rows, width), BF16),
            ((width, width), F32),
            ((width, width), BF16),
        ],
        [vmem()] * 3,
        [smem()] + [vmem()] * 7 + [any_spec()] * sum(counts),
        [
            pltpu.VMEM((blocks - early * rows, width), BF16),
            pltpu.VMEM((blocks + BLK, width), BF16),
            pltpu.VMEM((2 * rows, width), BF16),
            pltpu.VMEM((width, width), F32),
            pltpu.SemaphoreType.DMA((sum(counts) + 1,)),
        ],
        (plan, w_first, v_own, v_far, hg, hg_far, half, total)
        + tuple(p for g in groups for p in g),
        2 * dense,
    )

    keep, send = call(
        functools.partial(out_kernel, narrow),
        [((rows, width), F32), ((rows, width), BF16)],
        [vmem()] * 2,
        [vmem()] * 2,
        [],
        (mix, w_second),
        dense // 8,
    )

    part = gkeep + swap(gsend, "dom", 1).astype(F32)
    mine = feature(part, 0)
    for cx in range(1, nc):
        piece = swap(feature(part, cx).astype(BF16), "col", cx)
        mine = mine + piece.astype(F32)
    bit = 2
    while bit < nd:
        half = mine.astype(BF16)
        mine = half.astype(F32) + swap(half, "dom", bit).astype(F32)
        bit *= 2
    other = swap(mine, "dom", 1)
    grad_first, grad_second = call(
        last_kernel,
        [((width, narrow), F32)] * 2,
        [vmem()] * 2,
        [vmem()] * 2,
        [],
        (mine, other),
        width * narrow,
    )
    output = reduce_rows(keep, send)
    return output, grad_first, grad_second


def solution(mesh):
    in_specs = (
        P("dom", "col"),
        P(),
        P(),
        P("dom", None),
        P("dom"),
        P("dom", "col", None, None),
        P("dom", "col"),
    )
    out_specs = (P("dom", "col"), P(None, "col"), P(None, "col"))
    return jax.shard_map(work, mesh=mesh, in_specs=in_specs, out_specs=out_specs, check_vma=False)
```

```python
import functools

import jax
import jax.numpy as jnp
from jax import lax
from jax.experimental import pallas as pl
from jax.experimental.pallas import tpu as pltpu
from jax.sharding import PartitionSpec as P


BLK = 128
GROUP = 12
BACK = 4
PART = 512
LANES = 128
F32 = jnp.float32
BF16 = jnp.bfloat16


def swap(value, axis, mask):
    size = lax.axis_size(axis)
    return lax.ppermute(value, axis, [(i, i ^ mask) for i in range(size)])


def widen(own):
    if own.shape[1] % LANES:
        return lax.all_gather(own, "col", axis=1, tiled=True)
    return own


def gather_order(nd, nc):
    far = list(range(4, nd, 4))
    order = [(v, 0, (0, 0), "dom") for v in far[:2]]
    late = [(v, 0, (0, 0), "dom") for v in far[2:]]
    corners = []
    for n, v in enumerate((0, *far)):
        if nd >= 4:
            order.append((v | 2, 0, (v, 0), "dom"))
        order += [(v, cx, (v, 0), "col") for cx in range(1, nc)]
        order += late + corners
        late, corners = [], []
        for cx in range(1, nc):
            if nd >= 4 and (n + cx) % 2:
                corners.append((v | 2, cx, (v, cx), "dom"))
            elif nd >= 4:
                corners.append((v | 2, cx, (v | 2, 0), "col"))
    return order + corners


def gather(own, nc):
    nd = lax.axis_size("dom")
    got = {(0, 0): own}
    for v, cx, (sv, sc), axis in gather_order(nd, nc):
        mask = v ^ sv if axis == "dom" else cx ^ sc
        got[v, cx] = swap(got[sv, sc], axis, mask)
    return [[got[v, cx] for cx in range(nc)] for v in range(0, nd, 2)]


def load(groups, dest, sems, first=0):
    copies = []
    col = lax.axis_index("col")
    for g, pieces in enumerate(groups):
        for cx, piece in enumerate(pieces):
            rows, wide = piece.shape
            lane = 0
            if len(pieces) > 1:
                lane = pl.multiple_of((col ^ cx) * wide, LANES)
            copies.append(
                pltpu.make_async_copy(
                    piece,
                    dest.at[pl.ds(g * rows, rows), pl.ds(lane, wide)],
                    sems.at[first + len(copies)],
                )
            )
    for copy in copies:
        copy.start()
    return copies


def split(refs, counts):
    out, at = [], 0
    for n in counts:
        out.append(refs[at : at + n])
        at += n
    return out, refs[at:]


class Part:
    def __init__(self, ref, start):
        self.ref, self.start = ref, start

    def __getitem__(self, i):
        return self.ref[self.start + i]

    def __setitem__(self, i, value):
        self.ref[self.start + i] = value


def plan_size(nb, slots):
    return 2 * nb * (2 * (slots + GROUP) + 1)


def plan_parts(plan, nb, slots):
    size = 2 * nb * (slots + GROUP)
    return Part(plan, 0), Part(plan, size), Part(plan, 2 * size)


def tiles(vals, r, lk, at, count):
    return jnp.concatenate([vals[r, lk[at + t]] for t in range(count)], axis=1)


def place(lx, at):
    return pl.ds(pl.multiple_of(lx[at] * BLK, BLK), BLK)


def row_of(i, size):
    return pl.ds(pl.multiple_of(i * size, size), size)


def back_rows(nb, slots, first, lk, lx, ln, vals, cw, hg):
    def row(i, carry):
        grad = cw[row_of(i, BLK), :]
        base = (first + i) * (slots + GROUP)

        def step(g, carry):
            at = base + g * BACK
            prod = lax.dot_general(
                tiles(vals, i, lk, at, BACK),
                grad,
                (((0,), (0,)), ((), ())),
                preferred_element_type=F32,
            )
            for t in range(BACK):
                hg[place(lx, at + t), :] += prod[t * BLK : (t + 1) * BLK, :]
            return carry

        return lax.fori_loop(0, (ln[first + i] + BACK - 1) // BACK, step, carry)

    lax.fori_loop(0, nb, row, 0)


def project(cot, w2, cw):
    cw[...] = lax.dot_general(
        cot[...], w2[...], (((1,), (1,)), ((), ())), preferred_element_type=F32
    ).astype(BF16)


def back_kernel(nb, slots, counts, first, plan, w2, vals, *refs):
    groups, (hg, cot, cw, sems) = split(refs, counts)
    lk, lx, ln = plan_parts(plan, nb, slots)
    copies = load(groups, cot, sems)
    hg[...] = jnp.zeros_like(hg)
    for copy in copies:
        copy.wait()
    project(cot, w2, cw)
    back_rows(nb, slots, first, lk, lx, ln, vals, cw, hg)


def lists_kernel(nb, slots, blank, *refs):
    v_hbm, plan, v_own, cols_own, used_own, cols_far, used_far, sem = refs[4:]
    lk, lx, ln = plan_parts(plan, nb, slots)
    held = (cols_own, used_own, cols_far, used_far)
    scalars = [
        pltpu.make_async_copy(ref, here, sem.at[1 + n])
        for n, (ref, here) in enumerate(zip(refs[:4], held))
    ]
    for copy in scalars:
        copy.start()
    bring = pltpu.make_async_copy(v_hbm, v_own, sem.at[0])
    bring.start()
    for copy in scalars:
        copy.wait()
    dom = lax.axis_index("dom")
    base = lax.axis_index("col") * slots
    stride = slots + GROUP
    bits = nb.bit_length() - 1
    halves = ((cols_own, used_own), (cols_far, used_far))
    for half, (names, used) in enumerate(halves):

        def row(i, carry, half=half, names=names, used=used):
            start = (half * nb + i) * stride
            limit = used[i] - base
            n = start
            for k in range(slots):
                block = names[i, base + k]
                if nb == 1 << bits:
                    rel = block ^ (dom << bits)
                    ok = (rel & nb) == 0
                    spot = ((rel >> (bits + 1)) << bits) | (rel & (nb - 1))
                else:
                    rel = lax.div(block, jnp.int32(nb)) ^ dom
                    ok = (rel & 1) == 0
                    spot = (rel >> 1) * nb + lax.rem(block, jnp.int32(nb))
                lk[n] = k
                lx[n] = spot
                n = n + jnp.logical_and(k < limit, ok).astype(jnp.int32)
            ln[half * nb + i] = n - start
            for t in range(GROUP):
                lk[n + t] = 0
                lx[n + t] = blank
            return carry

        lax.fori_loop(0, nb, row, 0)
    bring.wait()


def put(ref, rows, value, narrow):
    width = value.shape[1]
    if narrow % LANES:
        ref[rows, :] = value.astype(ref.dtype)
        return
    col = lax.axis_index("col")
    for q in range(width // narrow):
        at = pl.ds(pl.multiple_of((col ^ q) * narrow, LANES), narrow)
        ref[rows, at] = value[:, q * narrow : (q + 1) * narrow].astype(ref.dtype)


def rows_product(slots, r, i, lk, lx, ln, vals, source, width):
    base = r * (slots + GROUP)

    def step(g, acc):
        at = base + g * GROUP
        right = jnp.concatenate(
            [source[place(lx, at + t), :] for t in range(GROUP)], axis=0
        )
        return acc + jnp.dot(
            tiles(vals, i, lk, at, GROUP), right, preferred_element_type=F32
        )

    steps = (ln[r] + GROUP - 1) // GROUP
    return lax.fori_loop(0, steps, step, jnp.zeros((BLK, width), F32))


def times_rows(nb, slots, first, plan, vals, source, ref, narrow):
    lk, lx, ln = plan_parts(plan, nb, slots)

    def row(i, carry):
        acc = rows_product(slots, first + i, i, lk, lx, ln, vals, source, source.shape[1])
        put(ref, row_of(i, BLK), acc, narrow)
        return carry

    lax.fori_loop(0, nb, row, 0)


def first_far_kernel(nb, slots, counts, narrow, plan, vals, *refs):
    groups, (src, send, sems) = split(refs, counts)
    copies = load(groups, src, sems)
    src[src.shape[0] - BLK :, :] = jnp.zeros((BLK, src.shape[1]), BF16)
    for copy in copies:
        copy.wait()
    times_rows(nb, slots, nb, plan, vals, src, send, narrow)


def first_own_kernel(nb, slots, narrow, plan, vals, src, keep):
    times_rows(nb, slots, 0, plan, vals, src, keep, narrow)


def activate(agg, w1, hg, hg_far, hid, total, places):
    for g in range(agg.shape[0] // PART):
        rows = pl.ds(g * PART, PART)
        there = pl.ds(places + g * PART, PART)
        a = agg[rows, :]
        first = jnp.dot(a, w1[...], preferred_element_type=F32)
        sig = 0.5 * jnp.tanh(0.5 * first) + 0.5
        act = first * sig
        hid[there, :] = act.astype(BF16)
        slope = sig + act * (1.0 - sig)
        grad = ((hg[there, :] + hg_far[there, :]) * slope).astype(BF16)
        total[...] += lax.dot_general(
            a, grad, (((0,), (0,)), ((), ())), preferred_element_type=F32
        )


def half_kernel(counts, w1, hg, hg_far, *refs):
    groups, (hid, total, agg, sems) = split(refs, counts)
    copies = load(groups, agg, sems)
    total[...] = jnp.zeros_like(total)
    for copy in copies:
        copy.wait()
    activate(agg, w1, hg, hg_far, hid, total, 0)


def second_kernel(
    nb, slots, counts, narrow, plan, w1, v_own, v_far, hg, hg_far, half, *refs
):
    lk, lx, ln = plan_parts(plan, nb, slots)
    part, *refs = refs
    groups, (mix, gkeep, gsend, agg, hid, cot, total, sems) = split(
        refs, counts
    )
    copies = load(groups[:-2], agg, sems)
    more = load(groups[-2:], cot, sems, len(copies))
    done = half.shape[0]
    bring = pltpu.make_async_copy(
        half, hid.at[pl.ds(0, done), :], sems.at[sum(counts)]
    )
    bring.start()
    blocks, width = done + agg.shape[0], agg.shape[1]
    chunk = nb * BLK
    hid[blocks:, :] = jnp.zeros((BLK, width), BF16)
    total[...] = part[...]
    for copy in copies:
        copy.wait()
    activate(agg, w1, hg, hg_far, hid, total, done)
    bring.wait()
    for half, vals in enumerate((v_own, v_far)):

        def row(i, carry, half=half, vals=vals):
            r = half * nb + i
            acc = rows_product(slots, r, i, lk, lx, ln, vals, hid, width)
            mix[row_of(r, BLK), :] = acc.astype(BF16)
            return carry

        lax.fori_loop(0, nb, row, 0)
    for copy in more:
        copy.wait()
    core = lax.axis_index("dom") & 1
    everything = pl.ds(0, width)
    second = lax.dot_general(
        mix[...], cot[...], (((0,), (0,)), ((), ())), preferred_element_type=F32
    )

    @pl.when(core == 0)
    def _():
        put(gkeep, everything, total[...], narrow)
        put(gsend, everything, second, narrow)

    @pl.when(core == 1)
    def _():
        put(gkeep, everything, second, narrow)
        put(gsend, everything, total[...], narrow)


def out_kernel(narrow, mix, w2, keep, send):
    chunk = keep.shape[0]
    for half, ref in enumerate((keep, send)):
        mine = mix[half * chunk : (half + 1) * chunk, :]
        value = jnp.dot(mine, w2[...], preferred_element_type=F32)
        put(ref, pl.ds(0, chunk), value, narrow)


def last_kernel(mine, other, grad_first, grad_second):
    core = lax.axis_index("dom") & 1

    @pl.when(core == 0)
    def _():
        grad_first[...] = mine[...]
        grad_second[...] = other[...]

    @pl.when(core == 1)
    def _():
        grad_first[...] = other[...]
        grad_second[...] = mine[...]


def any_spec():
    return pl.BlockSpec(memory_space=pl.ANY)


def vmem():
    return pl.BlockSpec(memory_space=pltpu.VMEM)


def smem():
    return pl.BlockSpec(memory_space=pltpu.SMEM)


def in_hbm(value):
    return pltpu.with_memory_space_constraint(value, pltpu.HBM)


def call(kernel, out, out_specs, in_specs, scratch, args, flops, grant=16):
    return pl.pallas_call(
        kernel,
        out_shape=tuple(jax.ShapeDtypeStruct(*o) for o in out),
        in_specs=in_specs,
        out_specs=tuple(out_specs),
        scratch_shapes=scratch,
        compiler_params=pltpu.CompilerParams(vmem_limit_bytes=grant << 20),
        cost_estimate=pl.CostEstimate(
            flops=flops, bytes_accessed=4 << 20, transcendentals=0
        ),
    )(*args)


def work(feats, w_first, w_second, block_cols, block_count, block_vals, cotangent):
    nd, nc = lax.axis_size("dom"), lax.axis_size("col")
    col = lax.axis_index("col")
    rows, narrow = feats.shape
    nb, slots = block_vals.shape[:2]
    width = narrow * nc
    blocks = nd // 2 * rows
    dense = 2 * 2 * nb * slots * BLK * BLK * width // 2

    pieces = 1 if narrow % LANES else nc
    chunks = gather(widen(feats), pieces)
    cot_own = [widen(cotangent)]
    for cx in range(1, pieces):
        cot_own.append(swap(cotangent, "col", cx))
    v_far = swap(block_vals, "dom", 1)
    cols = (
        block_cols, block_count, swap(block_cols, "dom", 1), swap(block_count, "dom", 1)
    )
    cot_far = [swap(piece, "dom", 1) for piece in cot_own]

    plan, v_own = call(
        functools.partial(lists_kernel, nb, slots, blocks // BLK),
        [
            ((plan_size(nb, slots),), jnp.int32),
            (block_vals.shape, BF16),
        ],
        [smem(), vmem()],
        [any_spec()] * 5,
        [
            pltpu.SMEM(block_cols.shape, jnp.int32),
            pltpu.SMEM(block_count.shape, jnp.int32),
            pltpu.SMEM(block_cols.shape, jnp.int32),
            pltpu.SMEM(block_count.shape, jnp.int32),
            pltpu.SemaphoreType.DMA((5,)),
        ],
        (*[in_hbm(c) for c in cols[:2]], *cols[2:], in_hbm(block_vals)),
        1 << 20,
    )

    counts = tuple(len(g) for g in chunks)
    if pieces > 1:
        chunks[0][0] = in_hbm(feats)
    src, send = call(
        functools.partial(first_far_kernel, nb, slots, counts, narrow),
        [((blocks + BLK, width), BF16), ((rows, width), BF16)],
        [vmem()] * 2,
        [smem(), vmem()] + [any_spec()] * sum(counts),
        [pltpu.SemaphoreType.DMA((sum(counts),))],
        (plan, v_far, *[p for g in chunks for p in g]),
        dense // 2,
    )
    (keep,) = call(
        functools.partial(first_own_kernel, nb, slots, narrow),
        [((rows, width), F32)],
        [vmem()],
        [smem(), vmem(), vmem()],
        [],
        (plan, v_own, src),
        dense // 2,
    )

    def back(first, vals, pieces):
        n = len(pieces)
        return call(
            functools.partial(back_kernel, nb, slots, (n,), first),
            [((blocks + BLK, width), F32)],
            [vmem()],
            [smem()] + [vmem()] * 2 + [any_spec()] * n,
            [
                pltpu.VMEM((rows, width), BF16),
                pltpu.VMEM((rows, width), BF16),
                pltpu.SemaphoreType.DMA((n,)),
            ],
            (plan, w_second, vals, *pieces),
            dense // 2,
        )[0]

    hg = back(0, v_own, cot_own)
    hg_far = back(nb, v_far, cot_far)

    def feature(value, cx):
        axis = value.ndim - 1
        if narrow % LANES:
            at = (col ^ cx) * narrow
            return lax.dynamic_slice_in_dim(value, at, narrow, axis)
        return lax.slice_in_dim(value, cx * narrow, (cx + 1) * narrow, axis=axis)

    def reduce_rows(keep, send):
        part = keep + swap(send, "dom", 1).astype(F32)
        total = feature(part, 0)
        for cx in range(1, nc):
            piece = feature(part, cx).astype(BF16)
            total = total + swap(piece, "col", cx).astype(F32)
        return total

    agg = reduce_rows(keep, send).astype(BF16)

    chunks = gather(widen(agg), pieces)
    early = (len(chunks) + 1) // 2
    counts = tuple(len(g) for g in chunks[:early])
    half, total = call(
        functools.partial(half_kernel, counts),
        [((early * rows, width), BF16), ((width, width), F32)],
        [vmem()] * 2,
        [vmem()] * 3 + [any_spec()] * sum(counts),
        [
            pltpu.VMEM((early * rows, width), BF16),
            pltpu.SemaphoreType.DMA((sum(counts),)),
        ],
        (w_first, hg, hg_far, *[p for g in chunks[:early] for p in g]),
        dense,
    )
    groups = chunks[early:] + [cot_own, cot_far]
    counts = tuple(len(g) for g in groups)
    mix, gkeep, gsend = call(
        functools.partial(second_kernel, nb, slots, counts, narrow),
        [
            ((2 * rows, width), BF16),
            ((width, width), F32),
            ((width, width), BF16),
        ],
        [vmem()] * 3,
        [smem()] + [vmem()] * 7 + [any_spec()] * sum(counts),
        [
            pltpu.VMEM((blocks - early * rows, width), BF16),
            pltpu.VMEM((blocks + BLK, width), BF16),
            pltpu.VMEM((2 * rows, width), BF16),
            pltpu.VMEM((width, width), F32),
            pltpu.SemaphoreType.DMA((sum(counts) + 1,)),
        ],
        (plan, w_first, v_own, v_far, hg, hg_far, half, total)
        + tuple(p for g in groups for p in g),
        2 * dense,
    )

    keep, send = call(
        functools.partial(out_kernel, narrow),
        [((rows, width), F32), ((rows, width), BF16)],
        [vmem()] * 2,
        [vmem()] * 2,
        [],
        (mix, w_second),
        dense // 8,
    )

    part = gkeep + swap(gsend, "dom", 1).astype(F32)

    def exchange(value, mask, axis="dom"):
        return swap(value, axis, mask).astype(F32)

    pieces = [feature(part, cx).astype(BF16) for cx in range(nc)]
    across = []
    if nd >= 4:
        both = ("dom", "col")
        for cx in range(1, nc):
            across.append(exchange(pieces[cx], 2 * nc + cx, both))
    mine = pieces[0].astype(F32)
    for cx in range(1, nc):
        mine = mine + exchange(pieces[cx], cx, "col")
    if nd >= 4:
        mine = mine + sum(across, exchange(pieces[0], 2))
    bit = 4
    while bit < nd:
        half = mine.astype(BF16)
        if 4 * bit <= nd:
            near, far = exchange(half, 2 * bit), exchange(half, 3 * bit)
            mine = (half.astype(F32) + exchange(half, bit)) + (near + far)
            bit *= 4
        else:
            mine = half.astype(F32) + exchange(half, bit)
            bit *= 2
    other = swap(mine, "dom", 1)
    grad_first, grad_second = call(
        last_kernel,
        [((width, narrow), F32)] * 2,
        [vmem()] * 2,
        [vmem()] * 2,
        [],
        (mine, other),
        width * narrow,
    )
    output = reduce_rows(keep, send)
    return output, grad_first, grad_second


def solution(mesh):
    in_specs = (
        P("dom", "col"),
        P(),
        P(),
        P("dom", None),
        P("dom"),
        P("dom", "col", None, None),
        P("dom", "col"),
    )
    out_specs = (P("dom", "col"), P(None, "col"), P(None, "col"))
    return jax.shard_map(work, mesh=mesh, in_specs=in_specs, out_specs=out_specs, check_vma=False)
```
